32 devices in a mesh: gx: 4 (over x, core), gy: 8 (over z, y).
Axes of the slice: x: 2, y: 2, z: 4, core: 2. Of those that a mesh axis runs over, the one named last changes fastest.
Arguments:
- sources: float32 [8, 4, 256, 1024], P('gy', 'gx'), may hold values from -6 to 6
- coeff_in: bfloat16 [8, 4, 256, 256], P('gy', 'gx'), may hold values from -0.375 to 0.375
- transfer: bfloat16 [8, 8, 4, 256, 512], P(None, 'gy', 'gx'), may hold values from -0.25 to 0.25
- coeff_out: bfloat16 [8, 4, 256, 256], P('gy', 'gx'), may hold values from -0.375 to 0.375
Outputs:
- targets: float32 [8, 4, 256, 1024], P('gy', 'gx')
The draws below stay inside these ranges and needn't reach their ends.
All inputs are finite; a program needn't handle non-finite values.
Results may differ from the reference program's by a relative error of at most 0.015.
Values may be sent and summed in bfloat16 or wider, within the bound.
A program may use at most 64 MiB of HBM per device.

```python
import jax
import jax.numpy as jnp
from jax import lax

RANK = 256
LEAF = 256
COLS = 1024
LEVELS = 8
N_GX = 4
N_GY = 8


def level_of(key, shape, pieces, smallest, top_value):
    def one(dim, shards_of):
        heights = jax.random.uniform(jax.random.fold_in(jax.random.fold_in(key, 6), dim), (shards_of,), jnp.float32, smallest / len(pieces), top_value / len(pieces))
        return jnp.repeat(jnp.exp(heights), shape[dim] // shards_of).reshape((-1,) + (1,) * (len(shape) - dim - 1))

    factor_of = one(*pieces[0])
    for cut in pieces[1:]:
        factor_of = factor_of * one(*cut)
    return factor_of


def noise(stream_key, dims, width, most, pieces=(), held_as=jnp.bfloat16):
    loudness = level_of(stream_key, dims, pieces, -0.22, 0.18) if pieces else 1.0
    entries = jax.random.normal(stream_key, dims, jnp.float32) * width * loudness
    return jnp.minimum(jnp.maximum(entries, -most), most).astype(held_as)


def setup_inputs(seed: int = 0) -> dict:
    key_list = jax.random.split(jax.random.key(seed), 5)
    sources = noise(key_list[0], (N_GY, N_GX, LEAF, COLS), 1.0, 6.0, ((0, 8), (1, 4)), jnp.float32)
    coeff_in = noise(key_list[1], (N_GY, N_GX, RANK, LEAF), LEAF ** -0.5, 0.375, ((0, 8), (1, 4)))
    transfer = noise(key_list[2], (LEVELS, N_GY, N_GX, RANK, 2 * RANK), (2 * RANK) ** -0.5, 0.25, ((1, 8), (2, 4)))
    coeff_out = noise(key_list[3], (N_GY, N_GX, LEAF, RANK), RANK ** -0.5, 0.375, ((0, 8), (1, 4)))
    return {"sources": sources, "coeff_in": coeff_in, "transfer": transfer, "coeff_out": coeff_out}


def apply_level(state, weights, level_bit):
    total = state.shape[0]
    block = 1 << level_bit
    groups = total // (2 * block)
    rank_rows = state.shape[1]
    cols_count = state.shape[2]
    shaped = state.reshape(groups, 2, block, rank_rows, cols_count)
    paired = jnp.concatenate([shaped[:, 0], shaped[:, 1]], axis=-2)
    paired = paired.reshape(groups * block, 2 * rank_rows, cols_count)
    wshape = weights.reshape(groups, 2, block, rank_rows, 2 * rank_rows)
    wshape = jnp.transpose(wshape, (0, 2, 1, 3, 4)).reshape(groups * block, 2 * rank_rows, 2 * rank_rows)

    def one_pair(items):
        return jnp.dot(items[0], items[1], preferred_element_type=jnp.float32).astype(jnp.bfloat16)

    result = lax.map(one_pair, (wshape, paired))
    result = result.reshape(groups, block, 2, rank_rows, cols_count)
    result = jnp.transpose(result, (0, 2, 1, 3, 4))
    return result.reshape(total, rank_rows, cols_count)


def reference(sources, coeff_in, transfer, coeff_out):
    total = N_GX * N_GY
    nbits = total.bit_length() - 1
    leaf_rows = sources.shape[2]
    cols_count = sources.shape[3]
    rank_rows = coeff_in.shape[2]
    source_flat = sources.reshape(total, leaf_rows, cols_count).astype(jnp.bfloat16)
    inward = coeff_in.reshape(total, rank_rows, leaf_rows)

    def compress(items):
        return jnp.dot(items[0], items[1], preferred_element_type=jnp.float32).astype(jnp.bfloat16)

    state = lax.map(compress, (inward, source_flat))
    for level in range(LEVELS):
        level_bit = nbits - 1 - (level % nbits)
        weights = transfer[level].reshape(total, rank_rows, 2 * rank_rows)
        state = apply_level(state, weights, level_bit)
    outward = coeff_out.reshape(total, leaf_rows, rank_rows)

    def expand(items):
        return jnp.dot(items[0], items[1], preferred_element_type=jnp.float32)

    result = lax.map(expand, (outward, state))
    return result.reshape(N_GY, N_GX, leaf_rows, cols_count)
```

```python
import functools

import jax
import jax.numpy as jnp
from jax import lax
from jax.experimental import pallas as pl
from jax.experimental.pallas import tpu as pltpu
from jax.sharding import PartitionSpec as P

MESH = pl.DeviceIdType.MESH
WIDTH = 128
LAGS = (0, 1, 2, 3, 4, 5, 6, 7, 8)


def kernel(
    low_bits,
    nbits,
    sources,
    coeff_in,
    transfer,
    coeff_out,
    targets,
    src,
    inward,
    weights,
    outward,
    pairs,
    result,
    load_sem,
    src_sem,
    out_sem,
    send_sem,
    recv_sem,
):
    levels = transfer.shape[0]
    rank = coeff_in.shape[0]
    chunks = sources.shape[1] // WIDTH
    axes = {"gx": lax.axis_index("gx"), "gy": lax.axis_index("gy")}

    def place(level):
        bit = nbits - 1 - level % nbits
        axis, mask = ("gx", 2**bit) if bit < low_bits else ("gy", 2 ** (bit - low_bits))
        index = axes[axis]
        side = index // mask % 2
        return side, {axis: index + mask * (1 - 2 * side)}

    places = [place(level) for level in range(levels)]

    def load_source(k):
        cols = pl.ds(k * WIDTH, WIDTH)
        return pltpu.make_async_copy(sources.at[:, cols], src.at[k], src_sem.at[k])

    def load_weights(level):
        return pltpu.make_async_copy(transfer.at[level], weights.at[level], load_sem.at[level])

    load_inward = pltpu.make_async_copy(coeff_in, inward, load_sem.at[levels])
    load_outward = pltpu.make_async_copy(coeff_out, outward, load_sem.at[levels + 1])

    def store_result(k):
        cols = pl.ds(k * WIDTH, WIDTH)
        return pltpu.make_async_copy(result.at[k], targets.at[:, cols], out_sem.at[k])

    def exchange(level, k):
        side, partner = places[level]
        half = pairs.at[level, k, pl.ds(pl.multiple_of(side * rank, rank), rank), :]
        return pltpu.make_async_remote_copy(
            src_ref=half,
            dst_ref=half,
            send_sem=send_sem.at[level, k],
            recv_sem=recv_sem.at[level, k],
            device_id=partner,
            device_id_type=MESH,
        )

    load_inward.start()
    for k in range(chunks):
        load_source(k).start()
    for level in range(levels):
        load_weights(level).start()
    load_outward.start()

    barrier = pltpu.get_barrier_semaphore()
    distinct = range(min(levels, nbits))
    for level in distinct:
        pl.semaphore_signal(barrier, inc=1, device_id=places[level][1], device_id_type=MESH)
    pl.semaphore_wait(barrier, len(distinct))

    def emit(level, k, total):
        side = places[level][0]
        pairs[level, k, pl.ds(pl.multiple_of(side * rank, rank), rank), :] = total.astype(jnp.bfloat16)
        exchange(level, k).start()

    def stage(s, k):
        if s == 0:
            load_source(k).wait()
            total = jnp.dot(
                inward[...], src[k].astype(jnp.bfloat16), preferred_element_type=jnp.float32
            )
            emit(0, k, total)
            return
        level = s - 1
        exchange(level, k).wait_recv()
        total = jnp.dot(weights[level], pairs[level, k], preferred_element_type=jnp.float32)
        if s < levels:
            emit(s, k, total)
            return
        state = total.astype(jnp.bfloat16)
        result[k] = jnp.dot(outward[...], state, preferred_element_type=jnp.float32)
        store_result(k).start()

    lags = LAGS
    for t in range(lags[levels] + chunks):
        for s in reversed(range(levels + 1)):
            k = t - lags[s]
            if k == 0:
                if s == 0:
                    load_inward.wait()
                else:
                    load_weights(s - 1).wait()
                if s == levels:
                    load_outward.wait()
            if 0 <= k < chunks:
                stage(s, k)

    for k in range(chunks):
        for level in range(levels):
            exchange(level, k).wait_send()
        store_result(k).wait()


def body(sources, coeff_in, transfer, coeff_out):
    low_bits = lax.axis_size("gx").bit_length() - 1
    nbits = low_bits + lax.axis_size("gy").bit_length() - 1
    levels, rank = transfer.shape[0], coeff_in.shape[2]
    leaf, cols = sources.shape[2:]
    chunks = cols // WIDTH
    result = pl.pallas_call(
        functools.partial(kernel, low_bits, nbits),
        out_shape=jax.ShapeDtypeStruct((leaf, cols), jnp.float32),
        in_specs=[pl.BlockSpec(memory_space=pl.ANY)] * 4,
        out_specs=pl.BlockSpec(memory_space=pl.ANY),
        scratch_shapes=[
            pltpu.VMEM((chunks, leaf, WIDTH), jnp.float32),
            pltpu.VMEM((rank, leaf), jnp.bfloat16),
            pltpu.VMEM((levels, rank, 2 * rank), jnp.bfloat16),
            pltpu.VMEM((leaf, rank), jnp.bfloat16),
            pltpu.VMEM((levels, chunks, 2 * rank, WIDTH), jnp.bfloat16),
            pltpu.VMEM((chunks, leaf, WIDTH), jnp.float32),
            pltpu.SemaphoreType.DMA((levels + 2,)),
            pltpu.SemaphoreType.DMA((chunks,)),
            pltpu.SemaphoreType.DMA((chunks,)),
            pltpu.SemaphoreType.DMA((levels, chunks)),
            pltpu.SemaphoreType.DMA((levels, chunks)),
        ],
        compiler_params=pltpu.CompilerParams(collective_id=0, has_side_effects=True),
        name="butterfly",
    )(sources[0, 0], coeff_in[0, 0], transfer[:, 0, 0], coeff_out[0, 0])
    return result[None, None]


def solution(mesh):
    placed = (
        P("gy", "gx", None, None),
        P("gy", "gx", None, None),
        P(None, "gy", "gx", None, None),
        P("gy", "gx", None, None),
    )
    return jax.shard_map(
        body, mesh=mesh, in_specs=placed, out_specs=P("gy", "gx", None, None), check_vma=False
    )
```

```python
import functools

import jax
import jax.numpy as jnp
from jax import lax
from jax.experimental import pallas as pl
from jax.experimental.pallas import tpu as pltpu
from jax.sharding import PartitionSpec as P

MESH = pl.DeviceIdType.MESH
WIDTH = 128
LAGS = (0, 2.1, 3.9, 5.3, 6.7, 7.4, 9.5, 11.3, 12.7)


def kernel(
    low_bits,
    nbits,
    sources,
    coeff_in,
    transfer,
    coeff_out,
    targets,
    src,
    inward,
    weights,
    outward,
    pairs,
    result,
    load_sem,
    src_sem,
    out_sem,
    send_sem,
    recv_sem,
):
    levels = transfer.shape[0]
    rank = coeff_in.shape[0]
    chunks = sources.shape[1] // WIDTH
    axes = {"gx": lax.axis_index("gx"), "gy": lax.axis_index("gy")}

    def place(level):
        bit = nbits - 1 - level % nbits
        axis, mask = ("gx", 2**bit) if bit < low_bits else ("gy", 2 ** (bit - low_bits))
        index = axes[axis]
        side = index // mask % 2
        return side, {axis: index + mask * (1 - 2 * side)}

    places = [place(level) for level in range(levels)]

    def load_source(k):
        cols = pl.ds(k * WIDTH, WIDTH)
        return pltpu.make_async_copy(sources.at[:, cols], src.at[k], src_sem.at[k])

    def load_weights(level):
        return pltpu.make_async_copy(transfer.at[level], weights.at[level], load_sem.at[level])

    load_inward = pltpu.make_async_copy(coeff_in, inward, load_sem.at[levels])
    load_outward = pltpu.make_async_copy(coeff_out, outward, load_sem.at[levels + 1])

    def store_result(k):
        cols = pl.ds(k * WIDTH, WIDTH)
        return pltpu.make_async_copy(result.at[k], targets.at[:, cols], out_sem.at[k])

    def exchange(level, k):
        side, partner = places[level]
        half = pairs.at[level, k, pl.ds(pl.multiple_of(side * rank, rank), rank), :]
        return pltpu.make_async_remote_copy(
            src_ref=half,
            dst_ref=half,
            send_sem=send_sem.at[level, k],
            recv_sem=recv_sem.at[level, k],
            device_id=partner,
            device_id_type=MESH,
        )

    load_inward.start()
    for k in range(chunks):
        load_source(k).start()
    for level in range(levels):
        load_weights(level).start()
    load_outward.start()

    barrier = pltpu.get_barrier_semaphore()
    distinct = range(min(levels, nbits))
    for level in distinct:
        pl.semaphore_signal(barrier, inc=1, device_id=places[level][1], device_id_type=MESH)
    pl.semaphore_wait(barrier, len(distinct))

    def emit(level, k, total):
        side = places[level][0]
        pairs[level, k, pl.ds(pl.multiple_of(side * rank, rank), rank), :] = total.astype(jnp.bfloat16)
        exchange(level, k).start()

    def stage(s, k):
        if s == 0:
            load_source(k).wait()
            total = jnp.dot(
                inward[...], src[k].astype(jnp.bfloat16), preferred_element_type=jnp.float32
            )
            emit(0, k, total)
            return
        level = s - 1
        exchange(level, k).wait_recv()
        total = jnp.dot(weights[level], pairs[level, k], preferred_element_type=jnp.float32)
        if s < levels:
            emit(s, k, total)
            return
        state = total.astype(jnp.bfloat16)
        result[k] = jnp.dot(outward[...], state, preferred_element_type=jnp.float32)
        store_result(k).start()

    turns = sorted((k + LAGS[s], -s, k) for s in range(levels + 1) for k in range(chunks))
    for _, minus, k in turns:
        s = -minus
        if k == 0:
            if s == 0:
                load_inward.wait()
            else:
                load_weights(s - 1).wait()
            if s == levels:
                load_outward.wait()
        stage(s, k)

    for k in range(chunks):
        for level in range(levels):
            exchange(level, k).wait_send()
        store_result(k).wait()


def body(sources, coeff_in, transfer, coeff_out):
    low_bits = lax.axis_size("gx").bit_length() - 1
    nbits = low_bits + lax.axis_size("gy").bit_length() - 1
    levels, rank = transfer.shape[0], coeff_in.shape[2]
    leaf, cols = sources.shape[2:]
    chunks = cols // WIDTH
    result = pl.pallas_call(
        functools.partial(kernel, low_bits, nbits),
        out_shape=jax.ShapeDtypeStruct((leaf, cols), jnp.float32),
        in_specs=[pl.BlockSpec(memory_space=pl.ANY)] * 4,
        out_specs=pl.BlockSpec(memory_space=pl.ANY),
        scratch_shapes=[
            pltpu.VMEM((chunks, leaf, WIDTH), jnp.float32),
            pltpu.VMEM((rank, leaf), jnp.bfloat16),
            pltpu.VMEM((levels, rank, 2 * rank), jnp.bfloat16),
            pltpu.VMEM((leaf, rank), jnp.bfloat16),
            pltpu.VMEM((levels, chunks, 2 * rank, WIDTH), jnp.bfloat16),
            pltpu.VMEM((chunks, leaf, WIDTH), jnp.float32),
            pltpu.SemaphoreType.DMA((levels + 2,)),
            pltpu.SemaphoreType.DMA((chunks,)),
            pltpu.SemaphoreType.DMA((chunks,)),
            pltpu.SemaphoreType.DMA((levels, chunks)),
            pltpu.SemaphoreType.DMA((levels, chunks)),
        ],
        compiler_params=pltpu.CompilerParams(collective_id=0, has_side_effects=True),
        name="butterfly",
    )(sources[0, 0], coeff_in[0, 0], transfer[:, 0, 0], coeff_out[0, 0])
    return result[None, None]


def solution(mesh):
    placed = (
        P("gy", "gx", None, None),
        P("gy", "gx", None, None),
        P(None, "gy", "gx", None, None),
        P("gy", "gx", None, None),
    )
    return jax.shard_map(
        body, mesh=mesh, in_specs=placed, out_specs=P("gy", "gx", None, None), check_vma=False
    )
```

```python
import functools

import jax
import jax.numpy as jnp
from jax import lax
from jax.experimental import pallas as pl
from jax.experimental.pallas import tpu as pltpu
from jax.sharding import PartitionSpec as P

MESH = pl.DeviceIdType.MESH
WIDTH = 128
TILES = 2
LAGS = (0, 2.1, 3.9, 5.3, 6.7, 7.4, 9.5, 11.3, 12.7)


def kernel(
    low_bits,
    nbits,
    sources,
    coeff_in,
    transfer,
    targets,
    src,
    inward,
    weights,
    pairs,
    result,
    load_sem,
    src_sem,
    out_sem,
    send_sem,
    recv_sem,
):
    levels = transfer.shape[0]
    rank = coeff_in.shape[0]
    chunks = sources.shape[1] // WIDTH
    axes = {"gx": lax.axis_index("gx"), "gy": lax.axis_index("gy")}

    def place(level):
        bit = nbits - 1 - level % nbits
        axis, mask = ("gx", 2**bit) if bit < low_bits else ("gy", 2 ** (bit - low_bits))
        index = axes[axis]
        side = index // mask % 2
        return side, {axis: index + mask * (1 - 2 * side)}

    places = [place(level) for level in range(levels)]

    def load_source(k):
        cols = pl.ds(k * WIDTH, WIDTH)
        return pltpu.make_async_copy(sources.at[:, cols], src.at[k], src_sem.at[k])

    def load_weights(level):
        return pltpu.make_async_copy(transfer.at[level], weights.at[level], load_sem.at[level])

    load_inward = pltpu.make_async_copy(coeff_in, inward, load_sem.at[levels])

    def store_result(k):
        cols = pl.ds(k * WIDTH, WIDTH)
        return pltpu.make_async_copy(result.at[k], targets.at[:, cols], out_sem.at[k])

    def exchange(level, k):
        side, partner = places[level]
        half = pairs.at[level, k, pl.ds(pl.multiple_of(side * rank, rank), rank), :]
        return pltpu.make_async_remote_copy(
            src_ref=half,
            dst_ref=half,
            send_sem=send_sem.at[level, k],
            recv_sem=recv_sem.at[level, k],
            device_id=partner,
            device_id_type=MESH,
        )

    load_inward.start()
    for k in range(chunks):
        load_source(k).start()
    for level in range(levels):
        load_weights(level).start()

    barrier = pltpu.get_barrier_semaphore()
    distinct = range(min(levels, nbits))
    for level in distinct:
        pl.semaphore_signal(barrier, inc=1, device_id=places[level][1], device_id_type=MESH)
    pl.semaphore_wait(barrier, len(distinct))

    def emit(level, k, total):
        side = places[level][0]
        pairs[level, k, pl.ds(pl.multiple_of(side * rank, rank), rank), :] = total.astype(jnp.bfloat16)
        exchange(level, k).start()

    def stage(s, k):
        if s == 0:
            load_source(k).wait()
            total = jnp.dot(
                inward[...], src[k].astype(jnp.bfloat16), preferred_element_type=jnp.float32
            )
            emit(0, k, total)
            return
        level = s - 1
        exchange(level, k).wait_recv()
        total = jnp.dot(weights[level], pairs[level, k], preferred_element_type=jnp.float32)
        if s < levels:
            emit(s, k, total)
            return
        state = total.astype(jnp.bfloat16)
        result[k] = state
        store_result(k).start()

    turns = sorted((k + LAGS[s], -s, k) for s in range(levels + 1) for k in range(chunks))
    for _, minus, k in turns:
        s = -minus
        if k == 0:
            if s == 0:
                load_inward.wait()
            else:
                load_weights(s - 1).wait()
        stage(s, k)

    for k in range(chunks):
        for level in range(levels):
            exchange(level, k).wait_send()
        store_result(k).wait()


def expand(outward, state, targets):
    targets[...] = jnp.dot(outward[...], state[...], preferred_element_type=jnp.float32)


def body(sources, coeff_in, transfer, coeff_out):
    low_bits = lax.axis_size("gx").bit_length() - 1
    nbits = low_bits + lax.axis_size("gy").bit_length() - 1
    levels, rank = transfer.shape[0], coeff_in.shape[2]
    leaf, cols = sources.shape[2:]
    chunks = cols // WIDTH
    state = pl.pallas_call(
        functools.partial(kernel, low_bits, nbits),
        out_shape=jax.ShapeDtypeStruct((rank, cols), jnp.bfloat16),
        in_specs=[pl.BlockSpec(memory_space=pl.ANY)] * 3,
        out_specs=pl.BlockSpec(memory_space=pl.ANY),
        scratch_shapes=[
            pltpu.VMEM((chunks, leaf, WIDTH), jnp.float32),
            pltpu.VMEM((rank, leaf), jnp.bfloat16),
            pltpu.VMEM((levels, rank, 2 * rank), jnp.bfloat16),
            pltpu.VMEM((levels, chunks, 2 * rank, WIDTH), jnp.bfloat16),
            pltpu.VMEM((chunks, rank, WIDTH), jnp.bfloat16),
            pltpu.SemaphoreType.DMA((levels + 1,)),
            pltpu.SemaphoreType.DMA((chunks,)),
            pltpu.SemaphoreType.DMA((chunks,)),
            pltpu.SemaphoreType.DMA((levels, chunks)),
            pltpu.SemaphoreType.DMA((levels, chunks)),
        ],
        compiler_params=pltpu.CompilerParams(collective_id=0, has_side_effects=True),
        name="butterfly",
    )(sources[0, 0], coeff_in[0, 0], transfer[:, 0, 0])
    tile = cols // TILES
    result = pl.pallas_call(
        expand,
        out_shape=jax.ShapeDtypeStruct((leaf, cols), jnp.float32),
        grid=(TILES,),
        in_specs=[
            pl.BlockSpec((leaf, rank), lambda i: (0, 0)),
            pl.BlockSpec((rank, tile), lambda i: (0, i)),
        ],
        out_specs=pl.BlockSpec((leaf, tile), lambda i: (0, i)),
        name="expand",
    )(coeff_out[0, 0], state)
    return result[None, None]


def solution(mesh):
    placed = (
        P("gy", "gx", None, None),
        P("gy", "gx", None, None),
        P(None, "gy", "gx", None, None),
        P("gy", "gx", None, None),
    )
    return jax.shard_map(
        body, mesh=mesh, in_specs=placed, out_specs=P("gy", "gx", None, None), check_vma=False
    )
```
